32 devices in a mesh: grp: 2 (over x), slc: 16 (over z, y, core).
Axes of the slice: x: 2, y: 2, z: 4, core: 2. Of those that a mesh axis runs over, the one named last changes fastest.
Arguments:
- bitstrings: int32 [1024], P('grp'), parts along dimension 0, may hold values from 0 to 511, as said below
- tree_order: int32 [12], P('grp'), parts along dimension 0, may hold values from 0 to 5, each once
- owners: int32 [12], P('grp'), parts along dimension 0, may hold values from 0 to 15
- slice_assign: int32 [64, 6], P(('grp', 'slc')), parts along dimension 0, may hold values from 0 to 63
- boundary: bfloat16 [1024, 4096], P('grp'), parts along dimension 0, may hold values from -6 to 6
- branch_pool: bfloat16 [32, 64, 4096], P(('grp', 'slc')), parts along dimension 0, may hold values from -0.75 to 0.75
- slice_tensors: bfloat16 [12, 64, 4096], P('grp'), parts along dimension 0, may hold values from -3 to 3
- closing: bfloat16 [8192, 128], P('grp'), parts along dimension 0, may hold values from -0.09375 to 0.09375
Outputs:
- amplitudes: float32 [1024, 128], P(('grp', 'slc')), parts along dimension 0
The draws below stay inside these ranges and needn't reach their ends.
There are 2 independent parts, one for each index of `grp`. The reference program is written for one: setup_inputs(seed, part) draws one part's arguments, and reference() takes and returns one part's arrays. A program takes and returns all parts, laid end to end along the dimension named above; each array names one. Nothing has to cross between parts.
Inputs may be any that keep to these rules, and one draw needn't show every extreme that they name: `bitstrings`: 512 distinct configurations. `tree_order`: a permutation of the sections.
All inputs are finite; a program needn't handle non-finite values.
Results may differ from the reference program's by a relative error of at most 0.0075.
Values may be sent and summed in bfloat16 or wider, within the bound.
A program may use at most 128 MiB of HBM per device.

```python
import math
import jax
import jax.numpy as jnp
from jax import lax

BOND = 64
PAIR = 4096
OUT = 128
NSTATES = 512
SECTIONS = 6
ROWS = 512
SLICES = 32
N_SLC = 16


def draw_bitstrings(key, part):
    key_middle = jax.random.fold_in(key, 11)
    key_order = jax.random.fold_in(key, 12)
    middle = jax.random.permutation(key_middle, NSTATES - 2)[:ROWS - 2].astype(jnp.int32) + 1
    ends = jnp.array([0, NSTATES - 1], jnp.int32)
    values = jnp.concatenate([ends, middle])
    order = jax.random.permutation(key_order, ROWS)
    return values[order].astype(jnp.int32)


def with_ends(values, rng, least, high):
    place = [jax.random.randint(jax.random.fold_in(rng, axis), (), 0, length) for axis, length in enumerate(values.shape)]
    longest = values.shape.index(max(values.shape))
    beside = place[:longest] + [(place[longest] + 1) % values.shape[longest]] + place[longest + 1:]
    return values.at[tuple(place)].set(least).at[tuple(beside)].set(high)


def level_of(key, dims, cuts, least, high):
    level = 1.0
    for position, shards_of in cuts:
        heights = jax.random.uniform(jax.random.fold_in(jax.random.fold_in(key, 6), position), (shards_of,), jnp.float32, least / len(cuts), high / len(cuts))
        level = level * jnp.repeat(jnp.exp(heights), dims[position] // shards_of).reshape((-1,) + (1,) * (len(dims) - 1 - position))
    return level


def scatter_about(rng, extent, deviation, bound, shards=(), kind=jnp.bfloat16):
    drawn = jax.random.normal(rng, extent, jnp.float32) * deviation
    if len(shards) > 0:
        drawn = level_of(rng, extent, shards, -0.22, 0.18) * drawn
    return jnp.clip(drawn, min=-bound, max=bound).astype(kind)


def setup_inputs(seed: int = 0, part: int = 0) -> dict:
    key_list = jax.random.split(jax.random.key(seed), 9)
    own_keys = jax.random.split(jax.random.fold_in(key_list[8], part), 9)
    return {
        "bitstrings": draw_bitstrings(jax.random.fold_in(jax.random.fold_in(key_list[8], part), 71), part),
        "tree_order": jax.random.permutation(own_keys[1], SECTIONS).astype(jnp.int32),
        "owners": with_ends(jax.random.randint(own_keys[2], (SECTIONS,), 0, N_SLC), jax.random.fold_in(own_keys[2], 1), 0, N_SLC - 1).astype(jnp.int32),
        "slice_assign": with_ends(jax.random.randint(own_keys[3], (SLICES, SECTIONS), 0, BOND), jax.random.fold_in(own_keys[3], 1), 0, BOND - 1).astype(jnp.int32),
        "boundary": scatter_about(own_keys[4], (NSTATES, PAIR), 1.0, 6.0),
        "branch_pool": scatter_about(own_keys[5], (N_SLC, BOND, PAIR), BOND ** -0.5, 0.75, ((0, 16),)),
        "slice_tensors": scatter_about(own_keys[6], (SECTIONS, BOND, PAIR), 1.0, 3.0),
        "closing": scatter_about(own_keys[7], (PAIR, OUT), PAIR ** -0.5, 0.09375),
    }


def reference(bitstrings, tree_order, owners, slice_assign, boundary, branch_pool, slice_tensors, closing):
    starts = jnp.take(boundary, bitstrings, axis=0)
    branches = jnp.take(branch_pool, owners, axis=0).astype(jnp.float32)

    def one_slice(assign):
        states = starts
        for section_idx in range(SECTIONS):
            product = jnp.einsum('rab,acb->rcb', states.astype(jnp.float32).reshape(ROWS, BOND, BOND), branches[section_idx].reshape(BOND, BOND, BOND))
            factor = slice_tensors[tree_order[section_idx], assign[section_idx]].astype(jnp.float32)
            states = (product.reshape(ROWS, PAIR) * factor[None, :]).astype(jnp.bfloat16)
        return jnp.dot(states, closing, preferred_element_type=jnp.float32)
    partial_amps = lax.map(one_slice, slice_assign)
    return lax.optimization_barrier(jnp.sum(partial_amps, axis=0)) * (1.0 / math.sqrt(SLICES))
```

```python
import functools
import math

import jax
import jax.numpy as jnp
from jax import lax
from jax.experimental import pallas as pl
from jax.experimental.pallas import tpu as pltpu
from jax.sharding import PartitionSpec as P

MESH = pl.DeviceIdType.MESH
F32 = jnp.float32
BF16 = jnp.bfloat16
LANES = 128


def dot(left, right, left_dim=1, right_dim=0):
    return lax.dot_general(
        left, right, (((left_dim,), (right_dim,)), ((), ())), preferred_element_type=F32
    )


def split(value):
    high = value.astype(BF16)
    return high, (value - high.astype(F32)).astype(BF16)


def contract(
    n, bond, inverse,
    tree_ref, owner_ref, bits_ref, assign_ref, boundary_hbm, branch_hbm, slices_hbm, closing_hbm,
    out_ref,
    own, perm, held, picks, picks_held, picks_all, rows_in, closing_in, chooser, chosen, starts,
    closing_own, weights, factors, state, total, parts, parts_held,
    load_sem, pick_send, pick_recv, piece_send, piece_recv, part_send, part_recv,
):
    me = lax.axis_index("slc")
    per = LANES // bond
    units = bond // per
    width = held.shape[1]
    lanes = width * LANES
    repeat = n * width // units
    shift = int(math.log2(per))
    low = int(math.log2(bond))
    first_unit = (me // repeat) * width
    row_blocks = boundary_hbm.shape[0]
    sections = tree_ref.shape[0]
    each = picks.shape[0]
    slice_count = picks_all.shape[0]
    out_dim = closing_in.shape[1]

    loads = [
        pltpu.make_async_copy(branch_hbm.at[0], own, load_sem.at[0]),
        pltpu.make_async_copy(boundary_hbm, rows_in.at[pl.ds(0, row_blocks)], load_sem.at[1]),
        pltpu.make_async_copy(
            slices_hbm, rows_in.at[pl.ds(row_blocks, slices_hbm.shape[0])], load_sem.at[2]
        ),
        pltpu.make_async_copy(closing_hbm, closing_in, load_sem.at[3]),
    ]
    for load in loads:
        load.start()

    barrier = pltpu.get_barrier_semaphore()

    def greet(step, carry):
        peer = lax.rem(me + step, n)
        pl.semaphore_signal(barrier, inc=1, device_id={"slc": peer}, device_id_type=MESH)
        return carry

    lax.fori_loop(1, n, greet, 0)

    picks[...] = jnp.zeros_like(picks)
    picks[:, 0:sections] = assign_ref[...]
    picks_held[me] = picks[...]

    loads[0].wait()
    lane16 = lax.broadcasted_iota(jnp.int32, (16, LANES), 1)

    def permute(step, carry):
        rows = pl.ds(pl.multiple_of(step * 16, 16), 16)
        cols = [own[rows, g * LANES : (g + 1) * LANES].astype(F32) for g in range(units)]
        bit = 1
        while bit < units:
            move = bit * per
            upper = (lane16 & move) != 0
            fresh = list(cols)
            for v in range(units):
                if v & bit == 0:
                    w = v + bit
                    fresh[v] = jnp.where(upper, pltpu.roll(cols[w], move, 1), cols[v])
                    fresh[w] = jnp.where(upper, cols[w], pltpu.roll(cols[v], LANES - move, 1))
            cols = fresh
            bit *= 2
        for u in range(units):
            perm[u, rows, :] = cols[u].astype(BF16)
        return carry

    lax.fori_loop(0, bond // 16, permute, 0)

    pl.semaphore_wait(barrier, n - 1)

    def pick_copy(step):
        return pltpu.make_async_remote_copy(
            src_ref=picks, dst_ref=picks_held.at[me],
            send_sem=pick_send.at[step], recv_sem=pick_recv.at[step],
            device_id={"slc": lax.rem(me + step, n)}, device_id_type=MESH,
        )

    def piece_copy(step):
        peer = lax.rem(me + step, n)
        return pltpu.make_async_remote_copy(
            src_ref=perm.at[pl.ds((peer // repeat) * width, width)], dst_ref=held.at[me],
            send_sem=piece_send.at[step], recv_sem=piece_recv.at[step],
            device_id={"slc": peer}, device_id_type=MESH,
        )

    def part_copy(step):
        peer = lax.rem(me + step, n)
        return pltpu.make_async_remote_copy(
            src_ref=parts.at[peer], dst_ref=parts_held.at[me],
            send_sem=part_send.at[step], recv_sem=part_recv.at[step],
            device_id={"slc": peer}, device_id_type=MESH,
        )

    def start_first(step, carry):
        pick_copy(step).start()
        piece_copy(step).start()
        return carry

    lax.fori_loop(1, n, start_first, 0)
    held[me] = perm[pl.ds(first_unit, width)]

    def lane_maps(shape, dim):
        lane = lax.broadcasted_iota(jnp.int32, shape, dim)
        group = (lane & (bond - 1)) >> shift
        half = (lane >> low) & (per - 1)
        local = (lane >> 7) * per + (lane & (per - 1))
        return group, half, local

    block = 2 * LANES
    group, half, local = lane_maps((block, lanes), 1)
    target = group * LANES + half * bond + first_unit * per + local
    target = target - lax.broadcasted_iota(jnp.int32, (block, lanes), 0)

    def build(step, carry):
        chooser[pl.ds(pl.multiple_of(step * block, block), block), :] = jnp.where(
            target == step * block, 1.0, 0.0
        ).astype(BF16)
        return carry

    lax.fori_loop(0, chooser.shape[0] // block, build, 0)
    for load in loads[1:]:
        load.wait()

    tall = rows_in.shape[0] // 2

    def choose(step, carry):
        part = rows_in[pl.ds(step * tall, tall)].reshape(tall * bond, rows_in.shape[2])
        chosen[pl.ds(step * tall, tall)] = dot(part, chooser[...]).astype(BF16).reshape(tall, bond, lanes)
        return carry

    lax.fori_loop(0, 2, choose, 0)
    closing_own[...] = dot(closing_in[...], chooser[...], 0, 0)

    row_total = row_blocks * bond
    order = lax.broadcasted_iota(jnp.int32, (row_total, row_total), 0) == bits_ref[...]
    starts[...] = dot(
        jnp.where(order, 1.0, 0.0).astype(BF16),
        chosen[0:row_blocks].reshape(row_total, lanes), 0, 0,
    ).astype(BF16)

    def end_pick(step, carry):
        pick_copy(step).wait()
        return carry

    lax.fori_loop(1, n, end_pick, 0)
    for idx in range(slice_count // each):
        picks_all[idx * each : (idx + 1) * each, :] = picks_held[idx * repeat + lax.rem(me, repeat)]
    values = lax.broadcasted_iota(jnp.int32, (slice_count, bond), 1)
    for k in range(sections):
        hot = jnp.where(values == picks_all[:, k : k + 1], 1.0, 0.0).astype(BF16)
        factors[k] = dot(hot, chosen[row_blocks + tree_ref[k]])

    for s in range(slice_count):
        state[s * out_dim : (s + 1) * out_dim, :] = (
            closing_own[...] * factors[sections - 1, s : s + 1, :]
        ).astype(BF16)

    group, half, local = lane_maps((bond, lanes), 1)
    expand = jnp.where(
        group * per + half == lax.broadcasted_iota(jnp.int32, (bond, lanes), 0), 1.0, 0.0
    ).astype(BF16)
    same = lane_maps((lanes, lanes), 0)[2] == lane_maps((lanes, lanes), 1)[2]

    def end_piece(step, carry):
        piece_copy(step).wait()
        return carry

    lax.fori_loop(1, n, end_piece, 0)
    for k in range(sections):
        piece = held[owner_ref[k]]
        piece = jnp.concatenate([piece[h] for h in range(width)], axis=1)
        weights[k] = jnp.where(same, dot(piece, expand, 0, 0), 0.0).astype(BF16)

    total[...] = jnp.zeros_like(total)
    some = min(8, slice_count)
    rows_of = some * out_dim

    def section(k, step):
        rows = pl.ds(pl.multiple_of(step * rows_of, rows_of), rows_of)
        product = dot(state[rows, :], weights[k])
        factor = factors[k - 1, pl.ds(pl.multiple_of(step * some, some), some), :]
        for t in range(some):
            piece = product[t * out_dim : (t + 1) * out_dim, :] * factor[t : t + 1, :]
            if k > 1:
                place = pl.ds(pl.multiple_of(step * rows_of + t * out_dim, out_dim), out_dim)
                state[place, :] = piece.astype(BF16)
            else:
                total[...] += piece

    for k in range(sections - 1, 0, -1):

        def one(step, carry, k=k):
            section(k, step)
            return carry

        lax.fori_loop(0, slice_count // some, one, 0)

    high, rest = split(total[...])
    head = dot(high, weights[0]) + dot(rest, weights[0])
    high, rest = split(head)
    amps = dot(starts[...], high, 1, 1) + dot(starts[...], rest, 1, 1)
    parts[...] = amps.reshape(parts.shape).astype(BF16)

    def start_part(step, carry):
        part_copy(step).start()
        return carry

    lax.fori_loop(1, n, start_part, 0)
    parts_held[me] = parts[me]

    def end_part(step, carry):
        part_copy(step).wait()
        return carry

    lax.fori_loop(1, n, end_part, 0)
    summed = parts_held[0].astype(F32)
    for idx in range(1, n):
        summed = summed + parts_held[idx].astype(F32)
    out_ref[...] = summed * inverse


def local(
    n, bitstrings, tree_order, owners, slice_assign, boundary, branch_pool, slice_tensors, closing
):
    each, sections = slice_assign.shape
    bond, pair = branch_pool.shape[1:]
    rows = bitstrings.shape[0]
    out_dim = closing.shape[1]
    per = LANES // bond
    units = bond // per
    width = max(1, units // n)
    repeat = n * width // units
    lanes = width * LANES
    slice_count = each * n // repeat
    share = rows // n
    row_blocks = boundary.shape[0] // bond
    blocks = row_blocks + sections
    vmem = pl.BlockSpec(memory_space=pltpu.VMEM)
    smem = pl.BlockSpec(memory_space=pltpu.SMEM)
    far = pl.BlockSpec(memory_space=pl.ANY)
    return pl.pallas_call(
        functools.partial(contract, n, bond, 1.0 / math.sqrt(each * n)),
        out_shape=jax.ShapeDtypeStruct((share, out_dim), F32),
        in_specs=[smem, smem, vmem, vmem, far, far, far, far],
        out_specs=vmem,
        scratch_shapes=[
            pltpu.VMEM((bond, pair), BF16),
            pltpu.VMEM((units, bond, LANES), BF16),
            pltpu.VMEM((n, width, bond, LANES), BF16),
            pltpu.VMEM((each, LANES), jnp.int32),
            pltpu.VMEM((n, each, LANES), jnp.int32),
            pltpu.VMEM((slice_count, LANES), jnp.int32),
            pltpu.VMEM((blocks, bond, pair), BF16),
            pltpu.VMEM((pair, out_dim), BF16),
            pltpu.VMEM((pair, lanes), BF16),
            pltpu.VMEM((blocks, bond, lanes), BF16),
            pltpu.VMEM((rows, lanes), BF16),
            pltpu.VMEM((out_dim, lanes), F32),
            pltpu.VMEM((sections, lanes, lanes), BF16),
            pltpu.VMEM((sections, slice_count, lanes), F32),
            pltpu.VMEM((slice_count * out_dim, lanes), BF16),
            pltpu.VMEM((out_dim, lanes), F32),
            pltpu.VMEM((n, share, out_dim), BF16),
            pltpu.VMEM((n, share, out_dim), BF16),
            pltpu.SemaphoreType.DMA((4,)),
            pltpu.SemaphoreType.DMA((n,)),
            pltpu.SemaphoreType.DMA((n,)),
            pltpu.SemaphoreType.DMA((n,)),
            pltpu.SemaphoreType.DMA((n,)),
            pltpu.SemaphoreType.DMA((n,)),
            pltpu.SemaphoreType.DMA((n,)),
        ],
        compiler_params=pltpu.CompilerParams(
            collective_id=0, has_side_effects=True, vmem_limit_bytes=56 * 2**20
        ),
        name="contract",
    )(
        tree_order,
        owners,
        bitstrings.reshape(1, rows),
        slice_assign,
        boundary.reshape(row_blocks, bond, pair),
        branch_pool,
        slice_tensors,
        closing,
    )


def solution(mesh):
    return jax.shard_map(
        functools.partial(local, mesh.shape["slc"]),
        mesh=mesh,
        in_specs=(
            P("grp"),
            P("grp"),
            P("grp"),
            P(("grp", "slc"), None),
            P("grp", None),
            P(("grp", "slc"), None, None),
            P("grp", None, None),
            P("grp", None),
        ),
        out_specs=P(("grp", "slc"), None),
        check_vma=False,
    )
```

```python
import functools
import math

import jax
import jax.numpy as jnp
from jax import lax
from jax.experimental import pallas as pl
from jax.experimental.pallas import tpu as pltpu
from jax.sharding import PartitionSpec as P

MESH = pl.DeviceIdType.MESH
F32 = jnp.float32
BF16 = jnp.bfloat16
LANES = 128


def dot(left, right, left_dim=1, right_dim=0):
    return lax.dot_general(
        left, right, (((left_dim,), (right_dim,)), ((), ())), preferred_element_type=F32
    )


def split(value):
    high = value.astype(BF16)
    return high, (value - high.astype(F32)).astype(BF16)


def contract(
    n, bond, inverse,
    tree_ref, owner_ref, bits_ref, assign_ref, boundary_hbm, branch_hbm, slices_hbm, closing_hbm,
    out_ref,
    own, perm, held, picks, picks_held, picks_all, rows_in, closing_in, chooser, chosen, starts,
    closing_own, weights, factors, state, amps, parts, parts_held,
    load_sem, pick_send, pick_recv, piece_send, piece_recv, part_send, part_recv,
):
    me = lax.axis_index("slc")
    per = LANES // bond
    units = bond // per
    width = len(held)
    lanes = width * LANES
    repeat = n * width // units
    shift = int(math.log2(per))
    low = int(math.log2(bond))
    first_unit = (me // repeat) * width
    row_blocks = boundary_hbm.shape[0]
    sections = tree_ref.shape[0]
    each = picks.shape[0]
    slice_count = picks_all.shape[0]
    out_dim = closing_in.shape[1]

    loads = [
        pltpu.make_async_copy(branch_hbm.at[0], own, load_sem.at[0]),
        pltpu.make_async_copy(boundary_hbm, rows_in.at[pl.ds(0, row_blocks)], load_sem.at[1]),
        pltpu.make_async_copy(
            slices_hbm, rows_in.at[pl.ds(row_blocks, slices_hbm.shape[0])], load_sem.at[2]
        ),
        pltpu.make_async_copy(closing_hbm, closing_in, load_sem.at[3]),
    ]
    for load in loads:
        load.start()

    barrier = pltpu.get_barrier_semaphore()

    def greet(step, carry):
        peer = lax.rem(me + step, n)
        pl.semaphore_signal(barrier, inc=1, device_id={"slc": peer}, device_id_type=MESH)
        return carry

    lax.fori_loop(1, n, greet, 0)

    picks[...] = jnp.zeros_like(picks)
    picks[:, 0:sections] = assign_ref[...]
    picks_held[me] = picks[...]

    loads[0].wait()
    lane16 = lax.broadcasted_iota(jnp.int32, (16, LANES), 1)

    def permute(step, carry):
        rows = pl.ds(pl.multiple_of(step * 16, 16), 16)
        cols = [own[rows, g * LANES : (g + 1) * LANES].astype(F32) for g in range(units)]
        bit = 1
        while bit < units:
            move = bit * per
            upper = (lane16 & move) != 0
            fresh = list(cols)
            for v in range(units):
                if v & bit == 0:
                    w = v + bit
                    fresh[v] = jnp.where(upper, pltpu.roll(cols[w], move, 1), cols[v])
                    fresh[w] = jnp.where(upper, cols[w], pltpu.roll(cols[v], LANES - move, 1))
            cols = fresh
            bit *= 2
        for u in range(units):
            perm[u, rows, :] = cols[u].astype(BF16)
        return carry

    lax.fori_loop(0, bond // 16, permute, 0)

    pl.semaphore_wait(barrier, n - 1)

    def pick_copy(step):
        return pltpu.make_async_remote_copy(
            src_ref=picks, dst_ref=picks_held.at[me],
            send_sem=pick_send.at[step], recv_sem=pick_recv.at[step],
            device_id={"slc": lax.rem(me + step, n)}, device_id_type=MESH,
        )

    def piece_copy(step, h):
        peer = lax.bitwise_xor(me, n - step)
        return pltpu.make_async_remote_copy(
            src_ref=perm.at[(peer // repeat) * width + h], dst_ref=held[h].at[me],
            send_sem=piece_send.at[h, step], recv_sem=piece_recv.at[h, step],
            device_id={"slc": peer}, device_id_type=MESH,
        )

    def part_copy(step):
        peer = lax.rem(me + step, n)
        return pltpu.make_async_remote_copy(
            src_ref=parts.at[peer], dst_ref=parts_held.at[me],
            send_sem=part_send.at[step], recv_sem=part_recv.at[step],
            device_id={"slc": peer}, device_id_type=MESH,
        )

    def start_pick(step, carry):
        pick_copy(step).start()
        return carry

    lax.fori_loop(1, n, start_pick, 0)
    for h in range(width):

        def start_piece(step, carry, h=h):
            piece_copy(step, h).start()
            return carry

        lax.fori_loop(1, n, start_piece, 0)
        held[h][me] = perm[first_unit + h]

    def lane_maps(shape, dim):
        lane = lax.broadcasted_iota(jnp.int32, shape, dim)
        group = (lane & (bond - 1)) >> shift
        half = (lane >> low) & (per - 1)
        local = (lane >> 7) * per + (lane & (per - 1))
        return group, half, local

    block = 2 * LANES
    group, half, local = lane_maps((block, lanes), 1)
    target = group * LANES + half * bond + first_unit * per + local
    target = target - lax.broadcasted_iota(jnp.int32, (block, lanes), 0)

    def build(step, carry):
        chooser[pl.ds(pl.multiple_of(step * block, block), block), :] = jnp.where(
            target == step * block, 1.0, 0.0
        ).astype(BF16)
        return carry

    lax.fori_loop(0, chooser.shape[0] // block, build, 0)
    for load in loads[1:]:
        load.wait()

    tall = rows_in.shape[0] // 2

    def choose(step, carry):
        part = rows_in[pl.ds(step * tall, tall)].reshape(tall * bond, rows_in.shape[2])
        chosen[pl.ds(step * tall, tall)] = dot(part, chooser[...]).astype(BF16).reshape(tall, bond, lanes)
        return carry

    lax.fori_loop(0, 2, choose, 0)
    closing_own[...] = dot(closing_in[...], chooser[...], 0, 0)

    row_total = row_blocks * bond
    order = lax.broadcasted_iota(jnp.int32, (row_total, row_total), 0) == bits_ref[...]
    starts[...] = dot(
        jnp.where(order, 1.0, 0.0).astype(BF16),
        chosen[0:row_blocks].reshape(row_total, lanes), 0, 0,
    ).astype(BF16)

    def end_pick(step, carry):
        pick_copy(step).wait()
        return carry

    lax.fori_loop(1, n, end_pick, 0)
    for idx in range(slice_count // each):
        picks_all[idx * each : (idx + 1) * each, :] = picks_held[idx * repeat + lax.rem(me, repeat)]
    values = lax.broadcasted_iota(jnp.int32, (slice_count, bond), 1)
    pairs = slice_count // 2
    for k in range(sections):
        hot = jnp.where(values == picks_all[:, k : k + 1], 1.0, 0.0).astype(BF16)
        factor = dot(hot, chosen[row_blocks + tree_ref[k]])
        for h in range(width):
            for p in range(2):
                factors[h, k, :, p * LANES : (p + 1) * LANES] = factor[
                    p * pairs : (p + 1) * pairs, h * LANES : (h + 1) * LANES
                ]

    for h in range(width):
        own_closing = closing_own[:, h * LANES : (h + 1) * LANES]
        own_closing = jnp.concatenate([own_closing, own_closing], axis=1)
        for s in range(pairs):
            state[h, s] = (own_closing * factors[h, sections - 1, s : s + 1, :]).astype(BF16)

    group, half, local = lane_maps((bond, LANES), 1)
    expand = jnp.where(
        group * per + half == lax.broadcasted_iota(jnp.int32, (bond, LANES), 0), 1.0, 0.0
    ).astype(BF16)
    same = lane_maps((LANES, LANES), 0)[2] == lane_maps((LANES, LANES), 1)[2]
    weights[...] = jnp.zeros_like(weights)

    for h in range(width):

        def end_piece(step, carry, h=h):
            piece_copy(step, h).wait()
            return carry

        lax.fori_loop(1, n, end_piece, 0)
        for k in range(sections - 1, -1, -1):
            weight = jnp.where(same, dot(held[h][owner_ref[k]], expand, 0, 0), 0.0).astype(BF16)
            for p in range(2):
                place = slice(p * LANES, (p + 1) * LANES)
                weights[k, place, place] = weight
        for k in range(sections - 1, 0, -1):
            sums = None
            for s in range(pairs):
                piece = dot(state[h, s], weights[k]) * factors[h, k - 1, s : s + 1, :]
                if k > 1:
                    state[h, s] = piece.astype(BF16)
                else:
                    sums = piece if sums is None else sums + piece
        sums = sums[:, 0:LANES] + sums[:, LANES:]
        weight = weights[0, 0:LANES, 0:LANES]
        high, rest = split(sums)
        high, rest = split(dot(high, weight) + dot(rest, weight))
        mine = starts[:, h * LANES : (h + 1) * LANES]
        amp = dot(
            jnp.concatenate([mine, mine], axis=1), jnp.concatenate([high, rest], axis=1), 1, 1
        )
        if h > 0:
            amp = amp + amps[...]
        if h < width - 1:
            amps[...] = amp
        else:
            parts[...] = amp.reshape(parts.shape).astype(BF16)

    def start_part(step, carry):
        part_copy(step).start()
        return carry

    lax.fori_loop(1, n, start_part, 0)
    parts_held[me] = parts[me]

    def end_part(step, carry):
        part_copy(step).wait()
        return carry

    lax.fori_loop(1, n, end_part, 0)
    summed = parts_held[0].astype(F32)
    for idx in range(1, n):
        summed = summed + parts_held[idx].astype(F32)
    out_ref[...] = summed * inverse


def local(
    n, bitstrings, tree_order, owners, slice_assign, boundary, branch_pool, slice_tensors, closing
):
    each, sections = slice_assign.shape
    bond, pair = branch_pool.shape[1:]
    rows = bitstrings.shape[0]
    out_dim = closing.shape[1]
    per = LANES // bond
    units = bond // per
    width = max(1, units // n)
    repeat = n * width // units
    lanes = width * LANES
    slice_count = each * n // repeat
    share = rows // n
    row_blocks = boundary.shape[0] // bond
    blocks = row_blocks + sections
    vmem = pl.BlockSpec(memory_space=pltpu.VMEM)
    smem = pl.BlockSpec(memory_space=pltpu.SMEM)
    far = pl.BlockSpec(memory_space=pl.ANY)
    return pl.pallas_call(
        functools.partial(contract, n, bond, 1.0 / math.sqrt(each * n)),
        out_shape=jax.ShapeDtypeStruct((share, out_dim), F32),
        in_specs=[smem, smem, vmem, vmem, far, far, far, far],
        out_specs=vmem,
        scratch_shapes=[
            pltpu.VMEM((bond, pair), BF16),
            pltpu.VMEM((units, bond, LANES), BF16),
            [pltpu.VMEM((n, bond, LANES), BF16)] * width,
            pltpu.VMEM((each, LANES), jnp.int32),
            pltpu.VMEM((n, each, LANES), jnp.int32),
            pltpu.VMEM((slice_count, LANES), jnp.int32),
            pltpu.VMEM((blocks, bond, pair), BF16),
            pltpu.VMEM((pair, out_dim), BF16),
            pltpu.VMEM((pair, lanes), BF16),
            pltpu.VMEM((blocks, bond, lanes), BF16),
            pltpu.VMEM((rows, lanes), BF16),
            pltpu.VMEM((out_dim, lanes), F32),
            pltpu.VMEM((sections, 2 * LANES, 2 * LANES), BF16),
            pltpu.VMEM((width, sections, slice_count // 2, 2 * LANES), F32),
            pltpu.VMEM((width, slice_count // 2, out_dim, 2 * LANES), BF16),
            pltpu.VMEM((rows, out_dim), F32),
            pltpu.VMEM((n, share, out_dim), BF16),
            pltpu.VMEM((n, share, out_dim), BF16),
            pltpu.SemaphoreType.DMA((4,)),
            pltpu.SemaphoreType.DMA((n,)),
            pltpu.SemaphoreType.DMA((n,)),
            pltpu.SemaphoreType.DMA((width, n)),
            pltpu.SemaphoreType.DMA((width, n)),
            pltpu.SemaphoreType.DMA((n,)),
            pltpu.SemaphoreType.DMA((n,)),
        ],
        compiler_params=pltpu.CompilerParams(
            collective_id=0, has_side_effects=True, vmem_limit_bytes=56 * 2**20
        ),
        name="contract",
    )(
        tree_order,
        owners,
        bitstrings.reshape(1, rows),
        slice_assign,
        boundary.reshape(row_blocks, bond, pair),
        branch_pool,
        slice_tensors,
        closing,
    )


def solution(mesh):
    return jax.shard_map(
        functools.partial(local, mesh.shape["slc"]),
        mesh=mesh,
        in_specs=(
            P("grp"),
            P("grp"),
            P("grp"),
            P(("grp", "slc"), None),
            P("grp", None),
            P(("grp", "slc"), None, None),
            P("grp", None, None),
            P("grp", None),
        ),
        out_specs=P(("grp", "slc"), None),
        check_vma=False,
    )
```
